32 devices in a mesh: keys: 8 (over z, x), heads: 4 (over y, core).
Axes of the slice: x: 2, y: 2, z: 4, core: 2. Of those that a mesh axis runs over, the one named last changes fastest.
Arguments:
- queries: bfloat16 [64, 64, 128], P(None, 'heads'), may hold values from -128 to 128
- keys: bfloat16 [131072, 8, 128], P('keys', 'heads'), may hold values from -4 to 4
- values: bfloat16 [131072, 8, 128], P('keys', 'heads'), may hold values from -6 to 6
- out_weight: bfloat16 [8192, 8192], P('heads', 'keys'), may hold values from -0.0625 to 0.0625
- probe: bfloat16 [8192], P('keys'), may hold values from -6 to 6
- knocked: int32 [64, 16], replicated, may hold values from 0 to 31
Outputs:
- readout: float32 [64, 32], P(None, 'keys')
- picked: float32 [64, 16], replicated
The draws below stay inside these ranges and needn't reach their ends.
All inputs are finite; a program needn't handle non-finite values.
Results may differ from the reference program's by a relative error of at most 0.0003.
Values sent between devices are 32-bit elements; how exact they have to be, the bound alone decides.
A program may use at most 128 MiB of HBM per device.

```python
import jax
import jax.numpy as jnp
from jax import lax

D = 8192
HEADS = 64
KV_HEADS = 8
HD = 128
NQ = 64
BLOCK = 4096
PICK = 16
BLOCKS = 32
CONTEXT = 131072


def masked_plan(key):
    count = max(1, min(3, NQ - 1))
    base = jax.random.fold_in(key, 31)
    askers = jax.random.permutation(jax.random.fold_in(base, 1), NQ - 1)[:count].astype(jnp.int32)
    offsets = jax.random.randint(jax.random.fold_in(base, 2), (count,), 0, NQ - 1 - askers)
    rows = CONTEXT - NQ + askers + 1 + offsets
    groups = jax.random.randint(jax.random.fold_in(base, 3), (count,), 0, KV_HEADS)
    within = jax.random.randint(jax.random.fold_in(base, 4), (count,), 0, HEADS // KV_HEADS)
    vectors = jnp.clip(jax.random.normal(jax.random.fold_in(base, 5), (count, HD), jnp.float32), -3.9, 3.9)
    return (rows, groups, within, askers, vectors)


def draw_keys(key, part):
    field = jnp.clip(jax.random.normal(jax.random.fold_in(key, 11), (CONTEXT, KV_HEADS, HD), jnp.float32), -4.0, 4.0)
    late_rows, late_groups, late_within, late_askers, late_vectors = masked_plan(key)
    field = field.at[late_rows, late_groups].set(late_vectors)
    return field.astype(jnp.bfloat16)


def draw_queries(key, part):
    field = 2.5 * jnp.clip(jax.random.normal(jax.random.fold_in(key, 21), (NQ, HEADS, HD), jnp.float32), -6.0, 6.0)
    late_rows, late_groups, late_within, late_askers, late_vectors = masked_plan(key)
    late_count = late_vectors.shape[0]
    late_strength = jnp.linspace(30.0, 60.0, late_count)
    late_scale = late_strength * HD ** 0.5 / jnp.sum(late_vectors * late_vectors, axis=1)
    late_heads = late_groups * (HEADS // KV_HEADS) + late_within
    field = field.at[late_askers, late_heads].set(late_scale[:, None] * late_vectors)
    field = jnp.clip(field, -128.0, 128.0)
    return field.astype(jnp.bfloat16)


def place_ends(values, own_key, low, largest):
    index_at = [jax.random.randint(jax.random.fold_in(own_key, axis), (), 0, length) for axis, length in enumerate(values.shape)]
    widest = values.shape.index(max(values.shape))
    next_to = index_at[:widest] + [(index_at[widest] + 1) % values.shape[widest]] + index_at[widest + 1:]
    return values.at[tuple(index_at)].set(low).at[tuple(next_to)].set(largest)


def block_levels(key, dims, cuts, low, largest):
    gain = 1.0
    for axis_at, blocks in cuts:
        draws = jax.random.uniform(jax.random.fold_in(jax.random.fold_in(key, 6), axis_at), (blocks,), jnp.float32, low / len(cuts), largest / len(cuts))
        gain = gain * jnp.repeat(jnp.exp(draws), dims[axis_at] // blocks).reshape((-1,) + (1,) * (len(dims) - 1 - axis_at))
    return gain


def gaussian(own_key, shape, scale, limit, cuts=(), held_as=jnp.bfloat16):
    gain = block_levels(own_key, shape, cuts, -0.22, 0.18) if cuts else 1.0
    drawn = jax.random.normal(own_key, shape, jnp.float32) * scale * gain
    return jnp.minimum(jnp.maximum(drawn, -limit), limit).astype(held_as)


def setup_inputs(seed: int = 0) -> dict:
    seeds = jax.random.split(jax.random.key(seed), 7)
    queries = draw_queries(jax.random.fold_in(seeds[6], 71), 0)
    keys = draw_keys(jax.random.fold_in(seeds[6], 71), 0)
    values = gaussian(seeds[2], (CONTEXT, KV_HEADS, HD), 1.0, 6.0, ((0, 8), (1, 4)))
    out_weight = gaussian(seeds[3], (HEADS * HD, D), (HEADS * HD) ** -0.5, 0.0625, ((0, 4), (1, 8)))
    probe = gaussian(seeds[4], (D,), 1.0, 6.0, ((0, 8),))
    knocked = place_ends(jax.random.randint(seeds[5], (NQ, PICK), 0, BLOCKS), jax.random.fold_in(seeds[5], 1), 0, BLOCKS - 1).astype(jnp.int32)
    return {"queries": queries, "keys": keys, "values": values, "out_weight": out_weight, "probe": probe, "knocked": knocked}


NEG = -1e30


def combine(first, second):
    m1, s1, o1 = first
    m2, s2, o2 = second
    top = jnp.maximum(m1, m2)
    a = jnp.exp(m1 - top)
    b = jnp.exp(m2 - top)
    return top, s1 * a + s2 * b, o1 * a[..., None] + o2 * b[..., None]


def reference(queries, keys, values, out_weight, probe, knocked):
    group = HEADS // KV_HEADS
    direction = jnp.dot(out_weight, probe, preferred_element_type=jnp.float32).reshape(KV_HEADS, group, HD)
    grouped = queries.astype(jnp.float32).reshape(NQ, KV_HEADS, group, HD)
    key_blocks = keys.reshape(BLOCKS, BLOCK, KV_HEADS, HD)
    value_blocks = values.reshape(BLOCKS, BLOCK, KV_HEADS, HD)
    query_pos = CONTEXT - NQ + jnp.arange(NQ, dtype=jnp.int32)

    def block_state(index):
        kblk = lax.dynamic_index_in_dim(key_blocks, index, 0, False).astype(jnp.float32)
        vblk = lax.dynamic_index_in_dim(value_blocks, index, 0, False).astype(jnp.float32)
        scores = jnp.einsum("qgrd,kgd->qgrk", grouped, kblk) * (HD ** -0.5)
        key_pos = index * BLOCK + jnp.arange(BLOCK, dtype=jnp.int32)
        allowed = key_pos[None, :] <= query_pos[:, None]
        scores = jnp.where(allowed[:, None, None, :], scores, NEG)
        top = jnp.max(scores, axis=-1)
        weights = jnp.exp(scores - top[..., None])
        total = jnp.sum(weights, axis=-1)
        summed = jnp.einsum("qgrk,kgd->qgrd", weights.astype(jnp.bfloat16).astype(jnp.float32), vblk)
        return top, total, summed

    states = lax.map(block_state, jnp.arange(BLOCKS, dtype=jnp.int32))
    empty = (jnp.full((NQ, KV_HEADS, group), NEG, jnp.float32),
             jnp.zeros((NQ, KV_HEADS, group), jnp.float32),
             jnp.zeros((NQ, KV_HEADS, group, HD), jnp.float32))

    def forward(carry, item):
        return combine(carry, item), carry

    _, before = lax.scan(forward, empty, states)
    _, after = lax.scan(forward, empty, states, reverse=True)
    top, total, summed = combine(before, after)
    projected = jnp.sum(summed * direction, axis=-1)
    readout = jnp.sum(projected / total, axis=(2, 3)).T
    picked = jnp.take_along_axis(readout, knocked, axis=1)
    return readout, picked
```

```python
import functools
import math

import jax
import jax.numpy as jnp
from jax import lax
from jax.experimental import pallas as pl
from jax.experimental.pallas import tpu as pltpu
from jax.sharding import PartitionSpec as P

BLOCK = 4096
NEG = -1e30
LANES = 128
CHUNK = 512
MESH = pl.DeviceIdType.MESH


def combine(first, second):
    m1, s1, o1 = first
    m2, s2, o2 = second
    top = jnp.maximum(m1, m2)
    a = jnp.exp(m1 - top)
    b = jnp.exp(m2 - top)
    return (top, s1 * a + s2 * b, o1 * a + o2 * b)


def exchange(size, axis, src, held, send, recv, start=True):
    me = lax.axis_index(axis)
    out = []
    for k in range(1, size):
        there = lax.rem(me + k, size)
        here = lax.rem(me + size - k, size)
        put = pltpu.make_async_remote_copy(src, held.at[me], send.at[k], recv.at[k], device_id={axis: there}, device_id_type=MESH)
        get = pltpu.make_async_remote_copy(src, held.at[here], send.at[k], recv.at[k], device_id={axis: there}, device_id_type=MESH)
        if start:
            put.start()
        out.append((put, get))
    return out


def finish(copies):
    for put, get in copies:
        get.wait_recv()
    for put, get in copies:
        put.wait_send()


def attend(lanes, hn, nblk, kvh, group, q_ref, k_ref, v_ref, w_ref, x_ref, all_ref,
           q2, pm, rel, sc, m_rep, m_run, s_run, o_all, cols, flip, st, tot, part, own,
           dirs, tots, reads, held, d_send, d_recv, t_send, t_recv, r_send, r_recv, g_send, g_recv):
    i = pl.program_id(0)
    nq, hq, hd = q_ref.shape
    rows = nq * group
    nchunk = k_ref.shape[0] // CHUNK
    tiles = CHUNK // LANES
    flat = rows // LANES
    scale = hd ** -0.5 * math.log2(math.e)
    device = lax.axis_index("keys")
    mine = lax.axis_index("heads")
    barrier = pltpu.get_barrier_semaphore()

    @pl.when(i == 0)
    def _():
        for k in range(1, lanes):
            pl.semaphore_signal(barrier, inc=1, device_id={"keys": lax.rem(device + k, lanes)}, device_id_type=MESH)
        for k in range(1, hn):
            pl.semaphore_signal(barrier, inc=1, device_id={"heads": lax.rem(mine + k, hn)}, device_id_type=MESH)
        q = q_ref[...].astype(jnp.float32)
        for h in range(kvh):
            piece = q[:, h * group:(h + 1) * group, :].reshape(rows, hd)
            q2[:, h * hd:(h + 1) * hd] = piece.astype(jnp.bfloat16)
        row = lax.broadcasted_iota(jnp.int32, (CHUNK, hd), 0)
        for h in range(kvh):
            pm[h] = jnp.where(lax.rem(row, kvh) == h, 1.0, 0.0).astype(jnp.bfloat16)
        r = lax.broadcasted_iota(jnp.int32, (rows, LANES), 0)
        c = lax.broadcasted_iota(jnp.int32, (rows, LANES), 1)
        rel[...] = (c // kvh + (CHUNK - LANES) // kvh) - r // group
        cols[...] = jnp.zeros_like(cols)

    def spread(ref, j):
        x = ref[pl.ds(pl.multiple_of(j * CHUNK, CHUNK), CHUNK), :]
        return jnp.concatenate([x * pm[h] for h in range(kvh)], axis=1)

    def score(j):
        s = lax.dot_general(q2[...], spread(k_ref, j), (((1,), (1,)), ((), ())), preferred_element_type=jnp.float32)
        base = (device * nblk + i) * BLOCK + j * (CHUNK // kvh)
        first = lanes * nblk * BLOCK - nq
        last = jnp.where(rel[...] <= first - base, s[:, CHUNK - LANES:], NEG)
        parts = [s[:, t * LANES:(t + 1) * LANES] for t in range(tiles - 1)] + [last]
        top = m_run[...]
        for t in range(tiles):
            sc[j, :, t * LANES:(t + 1) * LANES] = parts[t]
            top = jnp.maximum(top, parts[t])
        m_run[...] = top

    def weigh(j):
        m = m_rep[...]
        total = s_run[...]
        parts = []
        for t in range(tiles):
            p = jnp.exp2((sc[j, :, t * LANES:(t + 1) * LANES] - m) * scale)
            total = total + p
            parts.append(p.astype(jnp.bfloat16))
        s_run[...] = total
        o_all[i] += jnp.dot(jnp.concatenate(parts, axis=1), spread(v_ref, j), preferred_element_type=jnp.float32)

    lane = lax.broadcasted_iota(jnp.int32, (rows, LANES), 1)
    states = nblk * kvh
    some = lax.dot_general(jnp.broadcast_to(x_ref[...], (16, x_ref.shape[1])), w_ref[...], (((1,), (1,)), ((), ())),
                           preferred_element_type=jnp.float32)
    count = hq // nblk
    for t in range(count):
        part[pl.ds(i * count + t, 1), :] = some[0:1, t * hd:(t + 1) * hd]

    @pl.when(i == nblk - 1)
    def _():
        pl.semaphore_wait(barrier, lanes + hn - 2)
        exchange(lanes, "keys", part, dirs, d_send, d_recv, True)
        dirs[device] = part[...]

    m_run[...] = jnp.full_like(m_run, 2 * NEG)

    @pl.loop(0, nchunk)
    def _(j):
        score(j)

    run = m_run[...]
    out = jnp.zeros_like(run)
    acc = cols[...]
    for h in range(kvh):
        top = jnp.max(jnp.where(lax.rem(lane, kvh) == h, run, 2 * NEG), axis=1, keepdims=True)
        out = jnp.where(lax.rem(lane, kvh) == h, top, out)
        acc = jnp.where(lane == i * kvh + h, top * hd ** -0.5, acc)
    m_rep[...] = out
    s_run[...] = jnp.zeros_like(s_run)
    o_all[i] = jnp.zeros(o_all.shape[1:], jnp.float32)

    @pl.loop(0, nchunk)
    def _(j):
        weigh(j)

    for h in range(kvh):
        total = jnp.sum(jnp.where(lax.rem(lane, kvh) == h, s_run[...], 0.0), axis=1, keepdims=True)
        acc = jnp.where(lane == states + i * kvh + h, total, acc)
    cols[...] = acc

    @pl.when(i == nblk - 1)
    def _():
        finish(exchange(lanes, "keys", part, dirs, d_send, d_recv, False))
        direction = dirs[0]
        for k in range(1, lanes):
            direction = direction + dirs[k]
        acc = cols[...]
        for b in range(nblk):
            for h in range(kvh):
                o = o_all[b, :, h * hd:(h + 1) * hd].reshape(nq, group, hd) * direction[h * group:(h + 1) * group, :][None]
                o = jnp.sum(o.reshape(rows, hd), axis=1, keepdims=True)
                acc = jnp.where(lane == 2 * states + b * kvh + h, o, acc)
        flip[...] = acc.T
        for kind in range(3):
            for b in range(nblk):
                for h in range(kvh):
                    at = kind * states + b * kvh + h
                    for t in range(flat):
                        st[b, kind, h * flat + t:h * flat + t + 1, :] = flip[at:at + 1, t * LANES:(t + 1) * LANES]
        local = [tuple(st[b, kind] for kind in range(3)) for b in range(nblk)]
        whole = functools.reduce(combine, local)
        for kind in range(3):
            tot[kind] = whole[kind]
        copies = exchange(lanes, "keys", tot, tots, t_send, t_recv)
        shape = local[0][0].shape
        empty = (jnp.full(shape, NEG, jnp.float32), jnp.zeros(shape, jnp.float32), jnp.zeros(shape, jnp.float32))
        for kind in range(3):
            tots[device, kind] = empty[kind]
        finish(copies)
        outer = functools.reduce(combine, [tuple(tots[k, kind] for kind in range(3)) for k in range(lanes)])
        slim = lax.broadcasted_iota(jnp.int32, shape, 1)
        packed = jnp.zeros(shape, jnp.float32)
        for b in range(nblk):
            _, s, o = functools.reduce(combine, [local[c] for c in range(nblk) if c != b], outer)
            x = o / s
            step = 1
            while step < group:
                x = x + pltpu.roll(x, LANES - step, 1)
                step *= 2
            if b:
                x = pltpu.roll(x, b, 1)
            packed = jnp.where(lax.rem(slim, group) == b, x, packed)
        own[...] = functools.reduce(jnp.add, [packed[h * flat:(h + 1) * flat] for h in range(kvh)])
        copies = exchange(hn, "heads", own, reads, r_send, r_recv)
        reads[mine] = own[...]
        finish(copies)
        part[0:flat, :] = functools.reduce(jnp.add, [reads[k] for k in range(hn)])
        copies = exchange(lanes, "keys", part.at[pl.ds(0, flat)], held, g_send, g_recv)
        held[device] = part[0:flat, :]
        finish(copies)
        all_ref[...] = held[...]


def body(queries, keys, values, out_weight, probe, knocked):
    nq, hq, hd = queries.shape
    kvh = keys.shape[1]
    group = hq // kvh
    nblk = keys.shape[0] // BLOCK
    lanes = lax.axis_size("keys")
    hn = lax.axis_size("heads")
    device = lax.axis_index("keys")
    rows = nq * group
    flat = rows // LANES
    wide = BLOCK * kvh
    f32 = jnp.float32
    dma = pltpu.SemaphoreType.DMA
    every = pl.pallas_call(
        functools.partial(attend, lanes, hn, nblk, kvh, group),
        grid=(nblk,),
        in_specs=[
            pl.BlockSpec((nq, hq, hd), lambda i: (0, 0, 0)),
            pl.BlockSpec((wide, hd), lambda i: (i, 0)),
            pl.BlockSpec((wide, hd), lambda i: (i, 0)),
            pl.BlockSpec((hq * hd // nblk, out_weight.shape[1]), lambda i: (i, 0)),
            pl.BlockSpec((1, out_weight.shape[1]), lambda i: (0, 0)),
        ],
        out_specs=pl.BlockSpec(memory_space=pltpu.VMEM),
        out_shape=jax.ShapeDtypeStruct((lanes, flat, LANES), f32),
        scratch_shapes=[
            pltpu.VMEM((rows, kvh * hd), jnp.bfloat16),
            pltpu.VMEM((kvh, CHUNK, hd), jnp.bfloat16),
            pltpu.VMEM((rows, LANES), jnp.int32),
            pltpu.VMEM((wide // CHUNK, rows, CHUNK), f32),
            pltpu.VMEM((rows, LANES), f32),
            pltpu.VMEM((rows, LANES), f32),
            pltpu.VMEM((rows, LANES), f32),
            pltpu.VMEM((nblk, rows, kvh * hd), f32),
            pltpu.VMEM((rows, LANES), f32),
            pltpu.VMEM((LANES, rows), f32),
            pltpu.VMEM((nblk, 3, kvh * flat, LANES), f32),
            pltpu.VMEM((3, kvh * flat, LANES), f32),
            pltpu.VMEM((hq, hd), f32),
            pltpu.VMEM((flat, LANES), f32),
            pltpu.VMEM((lanes, hq, hd), f32),
            pltpu.VMEM((lanes, 3, kvh * flat, LANES), f32),
            pltpu.VMEM((hn, flat, LANES), f32),
            pltpu.VMEM((lanes, flat, LANES), f32),
            dma((lanes,)), dma((lanes,)), dma((lanes,)), dma((lanes,)),
            dma((hn,)), dma((hn,)), dma((lanes,)), dma((lanes,)),
        ],
        compiler_params=pltpu.CompilerParams(collective_id=0, has_side_effects=True, vmem_limit_bytes=60 * 2 ** 20),
    )(queries, keys.reshape(-1, hd), values.reshape(-1, hd), out_weight, probe.reshape(1, -1))
    every = every.reshape(lanes, nq, group)[:, :, :nblk]
    readout = lax.dynamic_index_in_dim(every, device, 0, False)
    table = jnp.swapaxes(every, 0, 1).reshape(nq, lanes * nblk)
    ids = jnp.arange(lanes * nblk, dtype=jnp.int32)
    picked = jnp.sum(jnp.where(knocked[:, :, None] == ids, table[:, None, :], 0.0), axis=-1)
    return (readout, picked)


def solution(mesh):
    in_specs = (
        P(None, "heads", None),
        P("keys", "heads", None),
        P("keys", "heads", None),
        P("heads", "keys"),
        P("keys"),
        P(),
    )
    out_specs = (P(None, "keys"), P())
    return jax.shard_map(body, mesh=mesh, in_specs=in_specs, out_specs=out_specs, check_vma=False)
```

```python
import functools
import math

import jax
import jax.numpy as jnp
from jax import lax
from jax.experimental import pallas as pl
from jax.experimental.pallas import tpu as pltpu
from jax.sharding import PartitionSpec as P

BLOCK = 4096
NEG = -1e30
LANES = 128
CHUNK = 2048
MESH = pl.DeviceIdType.MESH


def combine(first, second):
    m1, s1, o1 = first
    m2, s2, o2 = second
    top = jnp.maximum(m1, m2)
    a = jnp.exp(m1 - top)
    b = jnp.exp(m2 - top)
    return (top, s1 * a + s2 * b, o1 * a + o2 * b)


def exchange(size, axis, src, held, send, recv, start=True):
    me = lax.axis_index(axis)
    out = []
    for k in range(1, size):
        there = lax.rem(me + k, size)
        here = lax.rem(me + size - k, size)
        put = pltpu.make_async_remote_copy(src, held.at[me], send.at[k], recv.at[k], device_id={axis: there}, device_id_type=MESH)
        get = pltpu.make_async_remote_copy(src, held.at[here], send.at[k], recv.at[k], device_id={axis: there}, device_id_type=MESH)
        if start:
            put.start()
        out.append((put, get))
    return out


def finish(copies):
    for put, get in copies:
        get.wait_recv()
    for put, get in copies:
        put.wait_send()


def attend(lanes, hn, nblk, kvh, group, q_ref, k_ref, v_ref, w_ref, x_ref, all_ref,
           q2, pm, rel, sc, m_rep, m_run, s_run, o_all, cols, flip, st, tot, part, own,
           dirs, tots, reads, held, d_send, d_recv, t_send, t_recv, r_send, r_recv, g_send, g_recv):
    i = pl.program_id(0)
    nq, hq, hd = q_ref.shape
    rows = nq * group
    nchunk = k_ref.shape[0] // CHUNK
    tiles = CHUNK // LANES
    flat = rows // LANES
    scale = hd ** -0.5 * math.log2(math.e)
    device = lax.axis_index("keys")
    mine = lax.axis_index("heads")
    barrier = pltpu.get_barrier_semaphore()

    @pl.when(i == 0)
    def _():
        for k in range(1, lanes):
            pl.semaphore_signal(barrier, inc=1, device_id={"keys": lax.rem(device + k, lanes)}, device_id_type=MESH)
        for k in range(1, hn):
            pl.semaphore_signal(barrier, inc=1, device_id={"heads": lax.rem(mine + k, hn)}, device_id_type=MESH)
        q = q_ref[...].astype(jnp.float32)
        for h in range(kvh):
            piece = q[:, h * group:(h + 1) * group, :].reshape(rows, hd)
            q2[:, h * hd:(h + 1) * hd] = piece.astype(jnp.bfloat16)
        row = lax.broadcasted_iota(jnp.int32, (CHUNK, hd), 0)
        for h in range(kvh):
            pm[h] = jnp.where(lax.rem(row, kvh) == h, 1.0, 0.0).astype(jnp.bfloat16)
        r = lax.broadcasted_iota(jnp.int32, (rows, LANES), 0)
        c = lax.broadcasted_iota(jnp.int32, (rows, LANES), 1)
        rel[...] = (c // kvh + (CHUNK - LANES) // kvh) - r // group
        cols[...] = jnp.zeros_like(cols)

    def spread(ref, j):
        x = ref[pl.ds(pl.multiple_of(j * CHUNK, CHUNK), CHUNK), :]
        return jnp.concatenate([x * pm[h] for h in range(kvh)], axis=1)

    def score(j):
        s = lax.dot_general(q2[...], spread(k_ref, j), (((1,), (1,)), ((), ())), preferred_element_type=jnp.float32)
        base = (device * nblk + i) * BLOCK + j * (CHUNK // kvh)
        first = lanes * nblk * BLOCK - nq
        last = jnp.where(rel[...] <= first - base, s[:, CHUNK - LANES:], NEG)
        parts = [s[:, t * LANES:(t + 1) * LANES] for t in range(tiles - 1)] + [last]
        top = m_run[...]
        for t in range(tiles):
            sc[j, :, t * LANES:(t + 1) * LANES] = parts[t]
            top = jnp.maximum(top, parts[t])
        m_run[...] = top

    def weigh(j):
        m = m_rep[...]
        total = s_run[...]
        parts = []
        for t in range(tiles):
            p = jnp.exp2((sc[j, :, t * LANES:(t + 1) * LANES] - m) * scale)
            total = total + p
            parts.append(p.astype(jnp.bfloat16))
        s_run[...] = total
        o_all[i] += jnp.dot(jnp.concatenate(parts, axis=1), spread(v_ref, j), preferred_element_type=jnp.float32)

    lane = lax.broadcasted_iota(jnp.int32, (rows, LANES), 1)
    states = nblk * kvh
    some = lax.dot_general(jnp.broadcast_to(x_ref[...], (16, x_ref.shape[1])), w_ref[...], (((1,), (1,)), ((), ())),
                           preferred_element_type=jnp.float32)
    count = hq // nblk
    for t in range(count):
        part[pl.ds(i * count + t, 1), :] = some[0:1, t * hd:(t + 1) * hd]

    @pl.when(i == nblk - 1)
    def _():
        pl.semaphore_wait(barrier, lanes + hn - 2)
        exchange(lanes, "keys", part, dirs, d_send, d_recv, True)
        dirs[device] = part[...]

    m_run[...] = jnp.full_like(m_run, 2 * NEG)

    @pl.loop(0, nchunk)
    def _(j):
        score(j)

    run = m_run[...]
    out = jnp.zeros_like(run)
    acc = cols[...]
    for h in range(kvh):
        top = jnp.max(jnp.where(lax.rem(lane, kvh) == h, run, 2 * NEG), axis=1, keepdims=True)
        out = jnp.where(lax.rem(lane, kvh) == h, top, out)
        acc = jnp.where(lane == i * kvh + h, top * hd ** -0.5, acc)
    m_rep[...] = out
    s_run[...] = jnp.zeros_like(s_run)
    o_all[i] = jnp.zeros(o_all.shape[1:], jnp.float32)

    @pl.loop(0, nchunk)
    def _(j):
        weigh(j)

    for h in range(kvh):
        total = jnp.sum(jnp.where(lax.rem(lane, kvh) == h, s_run[...], 0.0), axis=1, keepdims=True)
        acc = jnp.where(lane == states + i * kvh + h, total, acc)
    cols[...] = acc

    @pl.when(i == nblk - 1)
    def _():
        finish(exchange(lanes, "keys", part, dirs, d_send, d_recv, False))
        direction = dirs[0]
        for k in range(1, lanes):
            direction = direction + dirs[k]
        acc = cols[...]
        for b in range(nblk):
            for h in range(kvh):
                o = o_all[b, :, h * hd:(h + 1) * hd].reshape(nq, group, hd) * direction[h * group:(h + 1) * group, :][None]
                o = jnp.sum(o.reshape(rows, hd), axis=1, keepdims=True)
                acc = jnp.where(lane == 2 * states + b * kvh + h, o, acc)
        flip[...] = acc.T
        for kind in range(3):
            for b in range(nblk):
                for h in range(kvh):
                    at = kind * states + b * kvh + h
                    for t in range(flat):
                        st[b, kind, h * flat + t:h * flat + t + 1, :] = flip[at:at + 1, t * LANES:(t + 1) * LANES]
        local = [tuple(st[b, kind] for kind in range(3)) for b in range(nblk)]
        whole = functools.reduce(combine, local)
        for kind in range(3):
            tot[kind] = whole[kind]
        copies = exchange(lanes, "keys", tot, tots, t_send, t_recv)
        shape = local[0][0].shape
        empty = (jnp.full(shape, NEG, jnp.float32), jnp.zeros(shape, jnp.float32), jnp.zeros(shape, jnp.float32))
        for kind in range(3):
            tots[device, kind] = empty[kind]
        finish(copies)
        outer = functools.reduce(combine, [tuple(tots[k, kind] for kind in range(3)) for k in range(lanes)])
        slim = lax.broadcasted_iota(jnp.int32, shape, 1)
        packed = jnp.zeros(shape, jnp.float32)
        for b in range(nblk):
            _, s, o = functools.reduce(combine, [local[c] for c in range(nblk) if c != b], outer)
            x = o / s
            step = 1
            while step < group:
                x = x + pltpu.roll(x, LANES - step, 1)
                step *= 2
            if b:
                x = pltpu.roll(x, b, 1)
            packed = jnp.where(lax.rem(slim, group) == b, x, packed)
        own[...] = functools.reduce(jnp.add, [packed[h * flat:(h + 1) * flat] for h in range(kvh)])
        copies = exchange(hn, "heads", own, reads, r_send, r_recv)
        reads[mine] = own[...]
        finish(copies)
        part[0:flat, :] = functools.reduce(jnp.add, [reads[k] for k in range(hn)])
        copies = exchange(lanes, "keys", part.at[pl.ds(0, flat)], held, g_send, g_recv)
        held[device] = part[0:flat, :]
        finish(copies)
        all_ref[...] = held[...]


def body(queries, keys, values, out_weight, probe, knocked):
    nq, hq, hd = queries.shape
    kvh = keys.shape[1]
    group = hq // kvh
    nblk = keys.shape[0] // BLOCK
    lanes = lax.axis_size("keys")
    hn = lax.axis_size("heads")
    device = lax.axis_index("keys")
    rows = nq * group
    flat = rows // LANES
    wide = BLOCK * kvh
    f32 = jnp.float32
    dma = pltpu.SemaphoreType.DMA
    every = pl.pallas_call(
        functools.partial(attend, lanes, hn, nblk, kvh, group),
        grid=(nblk,),
        in_specs=[
            pl.BlockSpec((nq, hq, hd), lambda i: (0, 0, 0)),
            pl.BlockSpec((wide, hd), lambda i: (i, 0)),
            pl.BlockSpec((wide, hd), lambda i: (i, 0)),
            pl.BlockSpec((hq * hd // nblk, out_weight.shape[1]), lambda i: (i, 0)),
            pl.BlockSpec((1, out_weight.shape[1]), lambda i: (0, 0)),
        ],
        out_specs=pl.BlockSpec(memory_space=pltpu.VMEM),
        out_shape=jax.ShapeDtypeStruct((lanes, flat, LANES), f32),
        scratch_shapes=[
            pltpu.VMEM((rows, kvh * hd), jnp.bfloat16),
            pltpu.VMEM((kvh, CHUNK, hd), jnp.bfloat16),
            pltpu.VMEM((rows, LANES), jnp.int32),
            pltpu.VMEM((wide // CHUNK, rows, CHUNK), f32),
            pltpu.VMEM((rows, LANES), f32),
            pltpu.VMEM((rows, LANES), f32),
            pltpu.VMEM((rows, LANES), f32),
            pltpu.VMEM((nblk, rows, kvh * hd), f32),
            pltpu.VMEM((rows, LANES), f32),
            pltpu.VMEM((LANES, rows), f32),
            pltpu.VMEM((nblk, 3, kvh * flat, LANES), f32),
            pltpu.VMEM((3, kvh * flat, LANES), f32),
            pltpu.VMEM((hq, hd), f32),
            pltpu.VMEM((flat, LANES), f32),
            pltpu.VMEM((lanes, hq, hd), f32),
            pltpu.VMEM((lanes, 3, kvh * flat, LANES), f32),
            pltpu.VMEM((hn, flat, LANES), f32),
            pltpu.VMEM((lanes, flat, LANES), f32),
            dma((lanes,)), dma((lanes,)), dma((lanes,)), dma((lanes,)),
            dma((hn,)), dma((hn,)), dma((lanes,)), dma((lanes,)),
        ],
        compiler_params=pltpu.CompilerParams(collective_id=0, has_side_effects=True, vmem_limit_bytes=60 * 2 ** 20),
    )(queries, keys.reshape(-1, hd), values.reshape(-1, hd), out_weight, probe.reshape(1, -1))
    every = every.reshape(lanes, nq, group)[:, :, :nblk]
    readout = lax.dynamic_index_in_dim(every, device, 0, False)
    table = jnp.swapaxes(every, 0, 1).reshape(nq, lanes * nblk)
    ids = jnp.arange(lanes * nblk, dtype=jnp.int32)
    picked = jnp.sum(jnp.where(knocked[:, :, None] == ids, table[:, None, :], 0.0), axis=-1)
    return (readout, picked)


def solution(mesh):
    in_specs = (
        P(None, "heads", None),
        P("keys", "heads", None),
        P("keys", "heads", None),
        P("heads", "keys"),
        P("keys"),
        P(),
    )
    out_specs = (P(None, "keys"), P())
    return jax.shard_map(body, mesh=mesh, in_specs=in_specs, out_specs=out_specs, check_vma=False)
```
